32 devices in a mesh: group: 2 (over y), ctx: 4 (over z), head: 2 (over x), dec: 2 (over core).
Axes of the slice: x: 2, y: 2, z: 4, core: 2. Of those that a mesh axis runs over, the one named last changes fastest.
Arguments:
- queries: bfloat16 [1024, 12288], P(('group', 'ctx'), ('head', 'dec')), parts along dimension 0, may hold values from -1100 to 1100
- latent_rows: bfloat16 [1024, 576], P(('group', 'ctx')), parts along dimension 0, may hold values from -8 to 8
- segments: int32 [1024], P('group'), parts along dimension 0, may hold values from 0 to 3, never falling along the last dimension, each value on 1 to 256 neighbouring positions
- owners: int32 [1024, 1], P(('group', 'ctx')), parts along dimension 0, may hold values from 0 to 7; in each aligned block of 128 rows (0 to 127, 128 to 255, ...) at most 32 rows name the same one
- absorb_key: bfloat16 [64, 128, 512], P(('head', 'dec')), may hold values from -0.5 to 0.5
- absorb_value: bfloat16 [64, 512, 128], P(('head', 'dec')), may hold values from -0.25 to 0.25
Outputs:
- attended: bfloat16 [1024, 8192], P(('group', 'ctx'), ('head', 'dec')), parts along dimension 0
- kv_cache: bfloat16 [16, 4, 32, 576], P(('group', 'ctx', 'dec')), parts along dimension 0
The draws below stay inside these ranges and needn't reach their ends.
There are 2 independent parts, one for each index of `group`. The reference program is written for one: setup_inputs(seed, part) draws one part's arguments, and reference() takes and returns one part's arrays. A program takes and returns all parts, laid end to end along the dimension named above; an argument that names none is the same for every part. Nothing has to cross between parts.
Inputs may be any that keep to these rules, and one draw needn't show every extreme that they name: `segments`: prompt numbers never fall along the tokens; each prompt has 1 to 256 tokens and one has exactly 256. `owners`: among the 128 tokens of one index of ctx no owner is named more than 32 times; some owner is named exactly 32 times in some of them; every owner is named somewhere.
All inputs are finite; a program needn't handle non-finite values.
Results may differ from the reference program's by a relative error of at most 0.0085.
Values may be sent and summed in bfloat16 or wider, within the bound.
A program may use at most 128 MiB of HBM per device.

```python
import math
import jax
import jax.numpy as jnp
import numpy as np
from jax import lax

NOPE = 128
ROPE = 64
LATENT = 512
VDIM = 128
HEADS = 64
DOCS = 4
TOK_DEV = 128
TOKENS = 512
OWNERS = 8
SLOT = 32
N_CTX = 4


def base_values(key, shape):
    return jnp.clip(jax.random.normal(key, shape, jnp.float32), -6.0, 6.0)


def shared_values(key):
    base_key = jax.random.fold_in(key, 7)
    split_keys = jax.random.split(base_key, 2)
    latent = base_values(split_keys[0], (TOKENS, LATENT + ROPE))
    query = base_values(split_keys[1], (TOKENS, HEADS, NOPE + ROPE))
    return (latent, query.reshape(TOKENS, HEADS * (NOPE + ROPE)))


def draw_queries(key, part):
    return shared_values(key)[1].astype(jnp.bfloat16)


def draw_latent_rows(key, part):
    return shared_values(key)[0].astype(jnp.bfloat16)


def shard_levels(own_key, dims, cuts, low, high):
    level, own = 1.0, jax.random.fold_in(own_key, 6)
    for position, parts in cuts:
        heights = jnp.exp(jax.random.uniform(jax.random.fold_in(own, position), (parts,), jnp.float32, low / len(cuts), high / len(cuts)))
        level = level * jnp.repeat(heights, dims[position] // parts).reshape([-1 if axis == position else 1 for axis in range(len(dims))])
    return level


def profile(amount, total, bound, skew):
    weights = [(1 << 20) // math.isqrt(grade ** skew) + 1 for grade in range(2, amount + 1)]
    rest, given = total - bound - (amount - 1), [1] * (amount - 1)
    while rest > 0:
        free = [i for i in range(amount - 1) if given[i] < bound]
        whole, budget = sum([weights[i] for i in free]), rest
        for i in free:
            more = min(bound - given[i], max(1, budget * weights[i] // whole), rest)
            given[i] = given[i] + more
            rest = rest - more
    return np.array([bound] + given)


def ragged(key, number_of, total, most, slope):
    if number_of == 2:
        one = jax.random.randint(key, (), max(1, total - most), min(most, total - 1) + 1)
        return jnp.stack([one, total - one])
    sizes = jnp.asarray(profile(number_of, total, most, slope), jnp.int32)
    pairs = (number_of - 1) // 2
    source_of, receiver = sizes[1:1 + 2 * pairs:2], sizes[2:2 + 2 * pairs:2]
    margin = jnp.minimum(source_of - 1, most - receiver)
    passed = jax.random.randint(jax.random.fold_in(key, 1), (pairs,), 0, 1 << 20) % (margin + 1)
    sizes = sizes.at[1:1 + 2 * pairs:2].set(source_of - passed).at[2:2 + 2 * pairs:2].set(receiver + passed)
    return sizes[jax.random.permutation(jax.random.fold_in(key, 2), number_of)]


def deal_out(key, own, number, rows, count, top, bound, slope):
    sequence = jax.random.permutation(key, count)
    heavy_load, usual = shares(count, rows * top, bound, slope, True), shares(count, rows * top, bound, slope, False)
    places = jnp.arange(count)

    def named(tallies, rotation):
        used = int((tallies > 0).sum())
        fixed = max(1, used // 4)
        shifted = fixed + (places - fixed + rotation * (used - fixed)) % max(1, count - fixed)
        return jnp.zeros((count,), jnp.int32).at[sequence[jnp.where(places < fixed, places, shifted)]].set(jnp.asarray(tallies, jnp.int32))

    tallies = jnp.where(number % 4 == 0, named(heavy_load, number // 4), named(usual, number - number // 4 - 1))
    mixed = jax.random.permutation(jax.random.fold_in(own, 3), count)
    source_of, receiver = mixed[0:count // 2 * 2:2], mixed[1:count // 2 * 2:2]
    margin = jnp.minimum(tallies[source_of] - 1, bound - tallies[receiver]) // 2
    margin = jnp.where((source_of == sequence[0]) | (receiver == sequence[0]) | (tallies[receiver] == 0), 0, jnp.maximum(margin, 0))
    shifted = jax.random.randint(jax.random.fold_in(own, 4), (count // 2,), 0, 1 << 20) % (margin + 1)
    tallies = tallies.at[source_of].add(-shifted).at[receiver].add(shifted)
    members = jnp.searchsorted(jnp.cumsum(tallies), jnp.arange(rows * top), side="right").astype(jnp.int32)
    table = members.reshape(top, rows).T
    table = table[jax.random.permutation(jax.random.fold_in(own, 1), rows)]
    rotation = jax.random.randint(jax.random.fold_in(own, 2), (rows, 1), 0, top)
    return jnp.take_along_axis(table, (jnp.arange(top)[None, :] + rotation) % top, axis=1)


def shares(number_of, total, bound, skew, full):
    loads = [(1 << 20) // math.isqrt(standing ** skew) + 1 for standing in range(1, number_of + 1)]
    largest = bound if full else min(bound, max(-(-total // number_of), total * loads[0] // sum(loads)))
    least = 1 if total - largest >= number_of - 1 else 0
    counts, spare = [largest] + [least] * (number_of - 1), total - largest - least * (number_of - 1)
    while spare > 0:
        candidates = [i for i in range(1, number_of) if counts[i] < largest] or [i for i in range(1, number_of) if counts[i] < bound]
        pool, remaining = sum([loads[i] for i in candidates]), spare
        for i in candidates:
            extra = min(bound - counts[i], max(1, remaining * loads[i] // pool), spare)
            counts[i] = counts[i] + extra
            spare = spare - extra
    return np.array(counts)


def centred(rng, dims, deviation, most, pieces=(), kind=jnp.bfloat16):
    drawn = deviation * jax.random.normal(rng, dims, jnp.float32)
    if pieces:
        drawn = drawn * shard_levels(rng, dims, pieces, -0.22, 0.18)
    return jnp.clip(drawn, -most, most).astype(kind)


def setup_inputs(seed: int = 0, part: int = 0) -> dict:
    arg_keys = jax.random.split(jax.random.key(seed), 7)
    part_keys = jax.random.split(jax.random.fold_in(arg_keys[6], part), 7)
    queries = draw_queries(jax.random.fold_in(jax.random.fold_in(arg_keys[6], part), 71), part)
    latent_rows = draw_latent_rows(jax.random.fold_in(jax.random.fold_in(arg_keys[6], part), 71), part)
    segments = jnp.searchsorted(jnp.cumsum(ragged(part_keys[2], DOCS, TOKENS, TOKENS // 2, 2)), jnp.arange(TOKENS), side="right").astype(jnp.int32)
    owners_keys = jax.random.split(jax.random.fold_in(part_keys[3], 1), TOKENS // TOK_DEV)
    owners_turns = jax.random.permutation(jax.random.fold_in(part_keys[3], 3), TOKENS // TOK_DEV)
    owners = jax.vmap(lambda own, number: deal_out(jax.random.fold_in(part_keys[3], 2), own, number, TOK_DEV, OWNERS, 1, SLOT, 2))(owners_keys, owners_turns).reshape((TOKENS, 1))
    absorb_key = centred(arg_keys[4], (HEADS, NOPE, LATENT), NOPE ** -0.5, 0.5, ((0, 4),))
    absorb_value = centred(arg_keys[5], (HEADS, LATENT, VDIM), LATENT ** -0.5, 0.25, ((0, 4),))
    return {"queries": queries, "latent_rows": latent_rows, "segments": segments, "owners": owners, "absorb_key": absorb_key, "absorb_value": absorb_value}


def rotate_pairs(rope_part, positions):
    half_rope = ROPE // 2
    frequency = 10000.0 ** (-jnp.arange(half_rope, dtype=jnp.float32) * 2.0 / ROPE)
    angles = positions.astype(jnp.float32)[:, None] * frequency[None, :]
    cosine = jnp.cos(angles)[:, None, :]
    sine_part = jnp.sin(angles)[:, None, :]
    first_part = rope_part[..., :half_rope]
    second = rope_part[..., half_rope:]
    return jnp.concatenate([first_part * cosine - second * sine_part, first_part * sine_part + second * cosine], axis=-1)


def reference(queries, latent_rows, segments, owners, absorb_key, absorb_value):
    width = LATENT + ROPE
    shaped = queries.reshape(TOKENS, HEADS, NOPE + ROPE)
    positions = jnp.arange(TOKENS, dtype=jnp.int32)
    rotated = rotate_pairs(shaped[..., NOPE:].astype(jnp.float32), positions).astype(jnp.bfloat16)
    absorbed = jnp.einsum("thn,hnc->thc", shaped[..., :NOPE].astype(jnp.float32), absorb_key.astype(jnp.float32)).astype(jnp.bfloat16)
    full_query = jnp.concatenate([absorbed, rotated], axis=-1)
    key_rows = latent_rows.astype(jnp.float32)
    values = key_rows[:, :LATENT]
    scale = (NOPE + ROPE) ** -0.5
    allowed = (positions[None, :] <= positions[:, None]) & (segments[None, :] == segments[:, None])

    def one_head(pair):
        query_head, value_map = pair
        scores = jnp.dot(query_head.astype(jnp.float32), key_rows.T, preferred_element_type=jnp.float32) * scale
        masked = jnp.where(allowed, scores, -1e30)
        row_max = jnp.max(masked, axis=1, keepdims=True)
        weights = jnp.where(allowed, jnp.exp(masked - row_max), 0.0)
        sums = jnp.sum(weights, axis=1, keepdims=True)
        mixed = jnp.dot(weights.astype(jnp.bfloat16).astype(jnp.float32), values, preferred_element_type=jnp.float32)
        latent_out = (mixed / sums).astype(jnp.bfloat16)
        return jnp.dot(latent_out.astype(jnp.float32), value_map.astype(jnp.float32), preferred_element_type=jnp.float32).astype(jnp.bfloat16)

    per_head = lax.map(one_head, (jnp.transpose(full_query, (1, 0, 2)), absorb_value))
    attended = jnp.transpose(per_head, (1, 0, 2)).reshape(TOKENS, HEADS * VDIM)

    owner_blocks = owners[:, 0].reshape(N_CTX, TOK_DEV)
    row_order = jnp.arange(TOK_DEV, dtype=jnp.int32)
    earlier = row_order[None, :] < row_order[:, None]
    same_owner = owner_blocks[:, :, None] == owner_blocks[:, None, :]
    slot_rank = jnp.sum(same_owner & earlier[None], axis=2).astype(jnp.int32)
    source = jnp.broadcast_to(jnp.arange(N_CTX, dtype=jnp.int32)[:, None], (N_CTX, TOK_DEV))
    kv_cache = jnp.zeros((OWNERS, N_CTX, SLOT, width), jnp.bfloat16)
    kv_cache = kv_cache.at[owner_blocks.reshape(-1), source.reshape(-1), slot_rank.reshape(-1)].set(latent_rows)
    return attended, kv_cache
```

```python
import functools

import jax
import jax.numpy as jnp
from jax import lax
from jax.experimental import pallas as pl
from jax.experimental.pallas import tpu as pltpu
from jax.sharding import PartitionSpec as P

NOPE = 128
ROPE = 64
LATENT = 512
VDIM = 128
MESH = pl.DeviceIdType.MESH
NEG = -1e30


def cdiv(a, b):
    return -(-a // b)


def kernel(
    n, cores, back, slots, chunk,
    freq_ref, seg_ref, owners_hbm, rows_hbm, q_hbm, ak_hbm, av_hbm,
    out_ref, kv_ref,
    qv, ak, av, qf, acc, m_ref, l_ref, held, owners,
    local_sem, send_sem, recv_sem, fsend_sem, frecv_sem, osend_sem, orecv_sem,
):
    c = lax.axis_index("ctx")
    d = lax.axis_index("dec")
    rows = rows_hbm.shape[0]
    heads = ak_hbm.shape[0]
    part = rows // cores
    scale = (NOPE + ROPE) ** (-0.5)
    last = n - 1

    loads = [
        pltpu.make_async_copy(rows_hbm, held.at[last], local_sem.at[0]),
        pltpu.make_async_copy(q_hbm, qv, local_sem.at[1]),
        pltpu.make_async_copy(ak_hbm, ak, local_sem.at[2]),
        pltpu.make_async_copy(av_hbm, av, local_sem.at[3]),
        pltpu.make_async_copy(owners_hbm, owners.at[last], local_sem.at[4]),
    ]
    for load in loads:
        load.start()

    barrier = pltpu.get_barrier_semaphore()
    for j in range(1, n):
        pl.semaphore_signal(
            barrier, inc=1, device_id={"ctx": lax.rem(c + j, n)}, device_id_type=MESH
        )
    for k in range(1, cores):
        pl.semaphore_signal(
            barrier, inc=1, device_id={"dec": lax.rem(d + k, cores)}, device_id_type=MESH
        )
    pl.semaphore_wait(barrier, n - 1 + cores - 1)

    mine = pl.ds(pl.multiple_of(d * part, part), part)
    sends = {}
    for j in range(1, n):
        target = {"ctx": lax.rem(c + j, n)}
        sends[j] = pltpu.make_async_remote_copy(
            src_ref=rows_hbm.at[mine],
            dst_ref=held.at[last - j, mine],
            send_sem=send_sem.at[j],
            recv_sem=recv_sem.at[j],
            device_id=target,
            device_id_type=MESH,
        )
        sends[j].start()
    osends = []
    for j in range(1, n):
        copy = pltpu.make_async_remote_copy(
            src_ref=owners_hbm,
            dst_ref=owners.at[last - j],
            send_sem=osend_sem.at[j],
            recv_sem=orecv_sem.at[j],
            device_id={"ctx": lax.rem(c + j, n)},
            device_id_type=MESH,
        )
        copy.start()
        osends.append(copy)

    forwards = {}

    def forward(j):
        sends[j].wait_recv()
        for k in range(1, cores):
            copy = pltpu.make_async_remote_copy(
                src_ref=held.at[last - j, mine],
                dst_ref=held.at[last - j, mine],
                send_sem=fsend_sem.at[j, k],
                recv_sem=frecv_sem.at[j, k],
                device_id={"dec": lax.rem(d + k, cores)},
                device_id_type=MESH,
            )
            copy.start()
            forwards[j, k] = copy

    lane = lax.broadcasted_iota(jnp.int32, (rows, 2 * ROPE), 1) % ROPE
    position = (lax.broadcasted_iota(jnp.int32, (rows, 2 * ROPE), 0) + c * rows).astype(jnp.float32)
    angles = position * freq_ref[0:1, :]
    low = lane < ROPE // 2
    cosine = jnp.cos(angles)
    sine = jnp.sin(angles)
    sine = jnp.where(low, -sine, sine)

    seg_now = seg_ref[pl.ds(c, 1), :].astype(jnp.float32)
    query_seg = jnp.transpose(jnp.broadcast_to(seg_now, (rows, rows)))
    row_id = lax.broadcasted_iota(jnp.int32, (rows, rows), 0)
    col_id = lax.broadcasted_iota(jnp.int32, (rows, rows), 1)

    def mask_of(j):
        key_seg = seg_ref[pl.ds(lax.rem(c - j + n, n), 1), :].astype(jnp.float32)
        same = query_seg == jnp.broadcast_to(key_seg, (rows, rows))
        if j == 0:
            return same & (col_id <= row_id)
        valid = jnp.broadcast_to(c, (rows, rows)) >= j
        return same & valid

    loads[1].wait()
    loads[2].wait()
    pair_width = 2 * (NOPE + ROPE)

    @pl.loop(0, heads // 2)
    def _(p):
        qp = qv[:, pl.ds(pl.multiple_of(p * pair_width, 128), pair_width)]
        rope = jnp.concatenate(
            [qp[:, NOPE:NOPE + ROPE], qp[:, 2 * NOPE + ROPE:]], axis=1
        ).astype(jnp.float32)
        swapped = jnp.where(
            low,
            pltpu.roll(rope, 2 * ROPE - ROPE // 2, 1),
            pltpu.roll(rope, ROPE // 2, 1),
        )
        rotated = (rope * cosine + swapped * sine).astype(jnp.bfloat16)
        qf[2 * p, :, LATENT:] = rotated[:, :ROPE]
        qf[2 * p + 1, :, LATENT:] = rotated[:, ROPE:]
        for k, start in ((0, 0), (1, NOPE + ROPE)):
            qf[2 * p + k, :, :LATENT] = jnp.dot(
                qp[:, start:start + NOPE], ak[2 * p + k], preferred_element_type=jnp.float32
            ).astype(jnp.bfloat16)

    if n > 1:
        forward(1)
    loads[0].wait()
    size = chunk * rows
    own_mask = mask_of(0)

    def scores_of(i, keys, mask):
        q = qf[pl.ds(i * chunk, chunk)].reshape(size, LATENT + ROPE)
        s = lax.dot_general(
            q, keys, (((1,), (1,)), ((), ())), preferred_element_type=jnp.float32
        )
        s = s.reshape(chunk, rows, keys.shape[0]) * scale
        return jnp.where(mask[None], s, NEG).reshape(size, keys.shape[0])

    def finish(i, total, sums):
        latent = (total / sums).astype(jnp.bfloat16)
        for k in range(chunk):
            h = i * chunk + k
            out_ref[:, pl.ds(pl.multiple_of(h * VDIM, VDIM), VDIM)] = jnp.dot(
                latent[k * rows:(k + 1) * rows], av[h], preferred_element_type=jnp.float32
            ).astype(jnp.bfloat16)

    @pl.loop(0, heads // chunk)
    def _(i):
        keys = held[last]
        s = scores_of(i, keys, own_mask)
        top = jnp.max(s, axis=1, keepdims=True)
        e = jnp.exp(s - top)
        at = pl.ds(pl.multiple_of(i * size, size), size)
        m_ref[at] = top
        l_ref[at] = jnp.sum(e, axis=1, keepdims=True)
        acc[at] = jnp.dot(
            e.astype(jnp.bfloat16), keys[:, :LATENT], preferred_element_type=jnp.float32
        )

    groups = [list(range(j, min(j + 2, back + 1))) for j in range(1, back + 1, 2)]
    waited = set()

    def settle(j):
        for k in range(1, cores):
            forwards[j, k].wait_recv()
        waited.add(j)

    loads[3].wait()
    for g, group in enumerate(groups):
        for j in group:
            if j > 1:
                forward(j)
        for j in group:
            settle(j)
        mask = jnp.concatenate([mask_of(j) for j in reversed(group)], axis=1)
        lo, hi = last - group[-1], last - group[0] + 1
        final = g == len(groups) - 1

        def step(i):
            keys = held[lo:hi].reshape((hi - lo) * rows, LATENT + ROPE)
            s = scores_of(i, keys, mask)
            at = pl.ds(pl.multiple_of(i * size, size), size)
            before = m_ref[at]
            top = jnp.maximum(before, jnp.max(s, axis=1, keepdims=True))
            e = jnp.exp(s - top)
            shrink = jnp.exp(before - top)
            sums = l_ref[at] * shrink + jnp.sum(e, axis=1, keepdims=True)
            total = acc[at] * shrink + jnp.dot(
                e.astype(jnp.bfloat16), keys[:, :LATENT], preferred_element_type=jnp.float32
            )
            if final:
                finish(i, total, sums)
            else:
                m_ref[at] = top
                l_ref[at] = sums
                acc[at] = total

        middle = (heads // chunk) // 2 if final else heads // chunk
        pl.loop(0, middle)(step)
        if final:
            for j in range(back + 1, n):
                forward(j)
            pl.loop(middle, heads // chunk)(step)

    for j in range(1, n):
        if j not in waited:
            settle(j)
    loads[4].wait()
    for copy in osends:
        copy.wait()

    me = c * cores + d
    before_tri = (row_id < col_id).astype(jnp.bfloat16)
    slot_id = lax.broadcasted_iota(jnp.int32, (slots, rows), 0).astype(jnp.float32)
    for j in range(n):
        named = owners[last - j, 0:8] == me
        rank = jnp.dot(
            named.astype(jnp.bfloat16), before_tri, preferred_element_type=jnp.float32
        )
        rank = jnp.where(named, rank, -1.0)
        picker = (jnp.broadcast_to(rank[0:1], (slots, rows)) == slot_id).astype(jnp.bfloat16)
        kv_ref[0, lax.rem(c - j + n, n)] = jnp.dot(
            picker, held[last - j], preferred_element_type=jnp.float32
        ).astype(jnp.bfloat16)

    for j in range(1, n):
        sends[j].wait_send()
        for k in range(1, cores):
            forwards[j, k].wait_send()


def on_device(sizes, queries, latent_rows, segments, owners, absorb_key, absorb_value):
    n, cores = sizes
    rows = latent_rows.shape[0]
    width = LATENT + ROPE
    heads = absorb_key.shape[0]
    tokens = segments.shape[0]
    back = min(n - 1, cdiv(tokens // 2 - 1, rows))
    slots = max(2, 2 * rows // (n * cores))
    chunk = 4
    frequency = 10000.0 ** (-jnp.arange(ROPE // 2, dtype=jnp.float32) * 2.0 / ROPE)
    frequency = jnp.broadcast_to(jnp.tile(frequency, 4)[None, :], (8, 2 * ROPE))
    segment_rows = segments.reshape(n, rows)
    owner_rows = jnp.broadcast_to(owners.reshape(1, rows), (8, rows))
    vmem = pl.BlockSpec(memory_space=pltpu.VMEM)
    hbm = pl.BlockSpec(memory_space=pl.ANY)
    dma = pltpu.SemaphoreType.DMA
    return tuple(pl.pallas_call(
        functools.partial(kernel, n, cores, back, slots, chunk),
        out_shape=(
            jax.ShapeDtypeStruct((rows, heads * VDIM), jnp.bfloat16),
            jax.ShapeDtypeStruct((1, n, slots, width), jnp.bfloat16),
        ),
        in_specs=[vmem, vmem, hbm, hbm, hbm, hbm, hbm],
        out_specs=(vmem, vmem),
        scratch_shapes=[
            pltpu.VMEM(queries.shape, jnp.bfloat16),
            pltpu.VMEM(absorb_key.shape, jnp.bfloat16),
            pltpu.VMEM(absorb_value.shape, jnp.bfloat16),
            pltpu.VMEM((heads, rows, width), jnp.bfloat16),
            pltpu.VMEM((heads * rows, LATENT), jnp.float32),
            pltpu.VMEM((heads * rows, 1), jnp.float32),
            pltpu.VMEM((heads * rows, 1), jnp.float32),
            pltpu.VMEM((n, rows, width), jnp.bfloat16),
            pltpu.VMEM((n, 8, rows), jnp.int32),
            dma((5,)),
            dma((n,)),
            dma((n,)),
            dma((n, cores)),
            dma((n, cores)),
            dma((n,)),
            dma((n,)),
        ],
        compiler_params=pltpu.CompilerParams(
            collective_id=0, has_side_effects=True, vmem_limit_bytes=48 * 1024 * 1024
        ),
    )(frequency, segment_rows, owner_rows, latent_rows, queries, absorb_key, absorb_value))


def solution(mesh):
    in_specs = (
        P(("group", "ctx"), ("head", "dec")),
        P(("group", "ctx"), None),
        P("group"),
        P(("group", "ctx"), None),
        P(("head", "dec"), None, None),
        P(("head", "dec"), None, None),
    )
    out_specs = (P(("group", "ctx"), ("head", "dec")), P(("group", "ctx", "dec"), None, None, None))
    sizes = (mesh.shape["ctx"], mesh.shape["dec"])
    return jax.shard_map(
        functools.partial(on_device, sizes),
        mesh=mesh, in_specs=in_specs, out_specs=out_specs, check_vma=False,
    )
```

```python
import functools

import jax
import jax.numpy as jnp
from jax import lax
from jax.experimental import pallas as pl
from jax.experimental.pallas import tpu as pltpu
from jax.sharding import PartitionSpec as P

NOPE = 128
ROPE = 64
LATENT = 512
VDIM = 128
MESH = pl.DeviceIdType.MESH
NEG = -1e30


def cdiv(a, b):
    return -(-a // b)


def kernel(
    n, cores, back, slots, chunk,
    freq_ref, seg_hbm, owners_hbm, rows_hbm, q_hbm, ak_hbm, av_hbm,
    out_ref, kv_ref,
    qv, ak, av, qf, acc, m_ref, l_ref, held, values, owners, seg_ref,
    local_sem, send_sem, recv_sem, fsend_sem, frecv_sem, osend_sem, orecv_sem,
):
    c = lax.axis_index("ctx")
    d = lax.axis_index("dec")
    rows = rows_hbm.shape[1]
    heads = ak_hbm.shape[0]
    part = (LATENT + ROPE) // cores
    scale = (NOPE + ROPE) ** (-0.5)
    last = n - 1

    loads = [
        pltpu.make_async_copy(rows_hbm, held.at[last], local_sem.at[0]),
        pltpu.make_async_copy(q_hbm, qv, local_sem.at[1]),
        pltpu.make_async_copy(ak_hbm, ak, local_sem.at[2]),
        pltpu.make_async_copy(av_hbm, av, local_sem.at[3]),
        pltpu.make_async_copy(owners_hbm, owners.at[last], local_sem.at[4]),
        pltpu.make_async_copy(seg_hbm, seg_ref, local_sem.at[5]),
    ]
    for load in loads:
        load.start()

    barrier = pltpu.get_barrier_semaphore()
    for j in range(1, n):
        pl.semaphore_signal(
            barrier, inc=1, device_id={"ctx": lax.rem(c + j, n)}, device_id_type=MESH
        )
    for k in range(1, cores):
        pl.semaphore_signal(
            barrier, inc=1, device_id={"dec": lax.rem(d + k, cores)}, device_id_type=MESH
        )
    pl.semaphore_wait(barrier, n - 1 + cores - 1)

    mine = pl.ds(pl.multiple_of(d * part, part), part)
    sends = {}
    for j in range(1, n):
        target = {"ctx": lax.rem(c + j, n)}
        sends[j] = pltpu.make_async_remote_copy(
            src_ref=rows_hbm.at[mine],
            dst_ref=held.at[last - j, mine],
            send_sem=send_sem.at[j],
            recv_sem=recv_sem.at[j],
            device_id=target,
            device_id_type=MESH,
        )
        sends[j].start()
    osends = []
    for j in range(1, n):
        copy = pltpu.make_async_remote_copy(
            src_ref=owners_hbm,
            dst_ref=owners.at[last - j],
            send_sem=osend_sem.at[j],
            recv_sem=orecv_sem.at[j],
            device_id={"ctx": lax.rem(c + j, n)},
            device_id_type=MESH,
        )
        copy.start()
        osends.append(copy)

    forwards = {}

    def forward(j):
        sends[j].wait_recv()
        for k in range(1, cores):
            copy = pltpu.make_async_remote_copy(
                src_ref=held.at[last - j, mine],
                dst_ref=held.at[last - j, mine],
                send_sem=fsend_sem.at[j, k],
                recv_sem=frecv_sem.at[j, k],
                device_id={"dec": lax.rem(d + k, cores)},
                device_id_type=MESH,
            )
            copy.start()
            forwards[j, k] = copy

    lane = lax.broadcasted_iota(jnp.int32, (rows, 2 * ROPE), 1) % ROPE
    position = (lax.broadcasted_iota(jnp.int32, (rows, 2 * ROPE), 0) + c * rows).astype(jnp.float32)
    angles = position * freq_ref[0:1, :]
    low = lane < ROPE // 2
    cosine = jnp.cos(angles)
    sine = jnp.sin(angles)
    sine = jnp.where(low, -sine, sine)

    loads[5].wait()
    seg_now = seg_ref[pl.ds(c, 1), :].astype(jnp.float32)
    query_seg = jnp.transpose(jnp.broadcast_to(seg_now, (rows, rows)))
    row_id = lax.broadcasted_iota(jnp.int32, (rows, rows), 0)
    col_id = lax.broadcasted_iota(jnp.int32, (rows, rows), 1)

    def mask_of(j):
        key_seg = seg_ref[pl.ds(lax.rem(c - j + n, n), 1), :].astype(jnp.float32)
        same = query_seg == jnp.broadcast_to(key_seg, (rows, rows))
        if j == 0:
            return same & (col_id <= row_id)
        valid = jnp.broadcast_to(c, (rows, rows)) >= j
        return same & valid

    loads[1].wait()
    loads[2].wait()
    pair_width = 2 * (NOPE + ROPE)

    @pl.loop(0, heads // 2)
    def _(p):
        qp = qv[:, pl.ds(pl.multiple_of(p * pair_width, 128), pair_width)]
        rope = jnp.concatenate(
            [qp[:, NOPE:NOPE + ROPE], qp[:, 2 * NOPE + ROPE:]], axis=1
        ).astype(jnp.float32)
        swapped = jnp.where(
            low,
            pltpu.roll(rope, 2 * ROPE - ROPE // 2, 1),
            pltpu.roll(rope, ROPE // 2, 1),
        )
        rotated = (rope * cosine + swapped * sine).astype(jnp.bfloat16)
        qf[2 * p, :, LATENT:] = rotated[:, :ROPE]
        qf[2 * p + 1, :, LATENT:] = rotated[:, ROPE:]
        for k, start in ((0, 0), (1, NOPE + ROPE)):
            qf[2 * p + k, :, :LATENT] = jnp.dot(
                qp[:, start:start + NOPE], ak[2 * p + k], preferred_element_type=jnp.float32
            ).astype(jnp.bfloat16)

    if n > 1:
        forward(1)
    loads[0].wait()
    size = chunk * rows
    own_mask = mask_of(0)

    def scores_of(i, keys, mask):
        q = qf[pl.ds(i * chunk, chunk)].reshape(size, LATENT + ROPE)
        s = jnp.dot(q, keys, preferred_element_type=jnp.float32)
        s = s.reshape(chunk, rows, keys.shape[1]) * scale
        return jnp.where(mask[None], s, NEG).reshape(size, keys.shape[1])

    def spread(j, at):
        values[at:at + rows] = jnp.transpose(held[last - j, :LATENT])

    def finish(i, total, sums):
        latent = (total / sums).astype(jnp.bfloat16)
        for k in range(chunk):
            h = i * chunk + k
            out_ref[:, pl.ds(pl.multiple_of(h * VDIM, VDIM), VDIM)] = jnp.dot(
                latent[k * rows:(k + 1) * rows], av[h], preferred_element_type=jnp.float32
            ).astype(jnp.bfloat16)

    spread(0, 0)

    @pl.loop(0, heads // chunk)
    def _(i):
        keys = held[last]
        s = scores_of(i, keys, own_mask)
        top = jnp.max(s, axis=1, keepdims=True)
        e = jnp.exp(s - top)
        at = pl.ds(pl.multiple_of(i * size, size), size)
        m_ref[at] = top
        l_ref[at] = jnp.sum(e, axis=1, keepdims=True)
        acc[at] = jnp.dot(
            e.astype(jnp.bfloat16), values[:rows], preferred_element_type=jnp.float32
        )

    groups = [list(range(j, min(j + 2, back + 1))) for j in range(1, back + 1, 2)]
    waited = set()

    def settle(j):
        for k in range(1, cores):
            forwards[j, k].wait_recv()
        waited.add(j)

    loads[3].wait()
    for g, group in enumerate(groups):
        for j in group:
            if j > 1:
                forward(j)
        for j in group:
            settle(j)
        mask = jnp.concatenate([mask_of(j) for j in reversed(group)], axis=1)
        for at, j in enumerate(reversed(group)):
            spread(j, at * rows)
        final = g == len(groups) - 1

        def step(i):
            keys = jnp.concatenate([held[last - j] for j in reversed(group)], axis=1)
            s = scores_of(i, keys, mask)
            at = pl.ds(pl.multiple_of(i * size, size), size)
            before = m_ref[at]
            top = jnp.maximum(before, jnp.max(s, axis=1, keepdims=True))
            e = jnp.exp(s - top)
            shrink = jnp.exp(before - top)
            sums = l_ref[at] * shrink + jnp.sum(e, axis=1, keepdims=True)
            total = acc[at] * shrink + jnp.dot(
                e.astype(jnp.bfloat16), values[:len(group) * rows],
                preferred_element_type=jnp.float32,
            )
            if final:
                finish(i, total, sums)
            else:
                m_ref[at] = top
                l_ref[at] = sums
                acc[at] = total

        middle = (heads // chunk) // 2 if final else heads // chunk
        pl.loop(0, middle)(step)
        if final:
            for j in range(back + 1, n):
                forward(j)
            pl.loop(middle, heads // chunk)(step)

    for j in range(1, n):
        if j not in waited:
            settle(j)
    loads[4].wait()
    for copy in osends:
        copy.wait()

    me = c * cores + d
    before_tri = (row_id < col_id).astype(jnp.bfloat16)
    slot_id = lax.broadcasted_iota(jnp.int32, (slots, rows), 0).astype(jnp.float32)
    for j in range(n):
        named = jnp.broadcast_to(owners[last - j], (8, rows)) == me
        rank = jnp.dot(
            named.astype(jnp.bfloat16), before_tri, preferred_element_type=jnp.float32
        )
        rank = jnp.where(named, rank, -1.0)
        picker = (jnp.broadcast_to(rank[0:1], (slots, rows)) == slot_id).astype(jnp.bfloat16)
        kv_ref[0, lax.rem(c - j + n, n)] = lax.dot_general(
            picker, held[last - j], (((1,), (1,)), ((), ())), preferred_element_type=jnp.float32
        ).astype(jnp.bfloat16)

    for j in range(1, n):
        sends[j].wait_send()
        for k in range(1, cores):
            forwards[j, k].wait_send()


def on_device(sizes, queries, latent_rows, segments, owners, absorb_key, absorb_value):
    n, cores = sizes
    rows = latent_rows.shape[0]
    width = LATENT + ROPE
    heads = absorb_key.shape[0]
    tokens = segments.shape[0]
    back = min(n - 1, cdiv(tokens // 2 - 1, rows))
    slots = max(2, 2 * rows // (n * cores))
    chunk = 4
    frequency = 10000.0 ** (-jnp.arange(ROPE // 2, dtype=jnp.float32) * 2.0 / ROPE)
    frequency = jnp.broadcast_to(jnp.tile(frequency, 4)[None, :], (8, 2 * ROPE))
    segment_rows = segments.reshape(n, rows)
    owner_rows = owners.reshape(1, rows)
    vmem = pl.BlockSpec(memory_space=pltpu.VMEM)
    hbm = pl.BlockSpec(memory_space=pltpu.HBM)
    dma = pltpu.SemaphoreType.DMA
    return tuple(pl.pallas_call(
        functools.partial(kernel, n, cores, back, slots, chunk),
        out_shape=(
            jax.ShapeDtypeStruct((rows, heads * VDIM), jnp.bfloat16),
            jax.ShapeDtypeStruct((1, n, slots, width), jnp.bfloat16),
        ),
        in_specs=[vmem, hbm, hbm, hbm, hbm, hbm, hbm],
        out_specs=(vmem, vmem),
        scratch_shapes=[
            pltpu.VMEM(queries.shape, jnp.bfloat16),
            pltpu.VMEM(absorb_key.shape, jnp.bfloat16),
            pltpu.VMEM(absorb_value.shape, jnp.bfloat16),
            pltpu.VMEM((heads, rows, width), jnp.bfloat16),
            pltpu.VMEM((heads * rows, LATENT), jnp.float32),
            pltpu.VMEM((heads * rows, 1), jnp.float32),
            pltpu.VMEM((heads * rows, 1), jnp.float32),
            pltpu.VMEM((n, width, rows), jnp.bfloat16),
            pltpu.VMEM((2 * rows, LATENT), jnp.bfloat16),
            pltpu.VMEM((n, 1, rows), jnp.int32),
            pltpu.VMEM((n, rows), jnp.int32),
            dma((6,)),
            dma((n,)),
            dma((n,)),
            dma((n, cores)),
            dma((n, cores)),
            dma((n,)),
            dma((n,)),
        ],
        compiler_params=pltpu.CompilerParams(
            collective_id=0, has_side_effects=True, vmem_limit_bytes=66200000
        ),
    )(frequency, segment_rows, owner_rows, latent_rows.T, queries, absorb_key, absorb_value))


def solution(mesh):
    in_specs = (
        P(("group", "ctx"), ("head", "dec")),
        P(("group", "ctx"), None),
        P("group"),
        P(("group", "ctx"), None),
        P(("head", "dec"), None, None),
        P(("head", "dec"), None, None),
    )
    out_specs = (P(("group", "ctx"), ("head", "dec")), P(("group", "ctx", "dec"), None, None, None))
    sizes = (mesh.shape["ctx"], mesh.shape["dec"])
    return jax.shard_map(
        functools.partial(on_device, sizes),
        mesh=mesh, in_specs=in_specs, out_specs=out_specs, check_vma=False,
    )
```

```python
import functools

import jax
import jax.numpy as jnp
import numpy as np
from jax import lax
from jax.experimental import pallas as pl
from jax.experimental.pallas import tpu as pltpu
from jax.sharding import PartitionSpec as P

NOPE = 128
ROPE = 64
LATENT = 512
VDIM = 128
MESH = pl.DeviceIdType.MESH
NEG = -1e30


def cdiv(a, b):
    return -(-a // b)


def kernel(
    n, cores, back, slots, chunk,
    freq_ref, seg_hbm, owners_hbm, rows_hbm, q_hbm, ak_hbm, av_hbm,
    out_ref, kv_ref,
    qv, ak, av, qf, acc, m_ref, l_ref, held, values, owners, seg_ref, compact,
    local_sem, send_sem, recv_sem, fsend_sem, frecv_sem, osend_sem, orecv_sem,
    ksend_sem, krecv_sem,
):
    c = lax.axis_index("ctx")
    d = lax.axis_index("dec")
    rows = rows_hbm.shape[1]
    heads = ak_hbm.shape[0]
    part = (LATENT + ROPE) // cores
    scale = (NOPE + ROPE) ** (-0.5)
    last = n - 1

    loads = [
        pltpu.make_async_copy(rows_hbm, held.at[last], local_sem.at[0]),
        pltpu.make_async_copy(q_hbm, qv, local_sem.at[1]),
        pltpu.make_async_copy(ak_hbm, ak, local_sem.at[2]),
        pltpu.make_async_copy(av_hbm, av, local_sem.at[3]),
        pltpu.make_async_copy(owners_hbm, owners.at[last], local_sem.at[4]),
        pltpu.make_async_copy(seg_hbm, seg_ref, local_sem.at[5]),
    ]
    for load in loads:
        load.start()

    barrier = pltpu.get_barrier_semaphore()
    for j in range(1, n):
        pl.semaphore_signal(
            barrier, inc=1, device_id={"ctx": lax.rem(c + j, n)}, device_id_type=MESH
        )
    for k in range(1, cores):
        pl.semaphore_signal(
            barrier, inc=1, device_id={"dec": lax.rem(d + k, cores)}, device_id_type=MESH
        )
    pl.semaphore_wait(barrier, n - 1 + cores - 1)

    mine = pl.ds(pl.multiple_of(d * part, part), part)
    sends, osends, ksends = {}, {}, {}
    for j in range(1, n):
        target = {"ctx": lax.rem(c + j, n)}
        ksends[j] = pltpu.make_async_remote_copy(
            src_ref=compact.at[j],
            dst_ref=kv_ref.at[0, c],
            send_sem=ksend_sem.at[j],
            recv_sem=krecv_sem.at[j],
            device_id=target,
            device_id_type=MESH,
        )
        if j > back:
            continue
        sends[j] = pltpu.make_async_remote_copy(
            src_ref=rows_hbm.at[mine],
            dst_ref=held.at[last - j, mine],
            send_sem=send_sem.at[j],
            recv_sem=recv_sem.at[j],
            device_id=target,
            device_id_type=MESH,
        )
        osends[j] = pltpu.make_async_remote_copy(
            src_ref=owners_hbm,
            dst_ref=owners.at[last - j],
            send_sem=osend_sem.at[j],
            recv_sem=orecv_sem.at[j],
            device_id=target,
            device_id_type=MESH,
        )

    for j in sends:
        @pl.when(c + j < n)
        def _():
            sends[j].start()
    for j in sends:
        @pl.when(c + j < n)
        def _():
            osends[j].start()

        @pl.when(c < j)
        def _():
            held[last - j] = jnp.zeros_like(held[last - j])

    forwards = {}
    for j in sends:
        for k in range(1, cores):
            forwards[j, k] = pltpu.make_async_remote_copy(
                src_ref=held.at[last - j, mine],
                dst_ref=held.at[last - j, mine],
                send_sem=fsend_sem.at[j, k],
                recv_sem=frecv_sem.at[j, k],
                device_id={"dec": lax.rem(d + k, cores)},
                device_id_type=MESH,
            )

    def forward(j):
        @pl.when(c >= j)
        def _():
            sends[j].wait_recv()
            for k in range(1, cores):
                forwards[j, k].start()

    lane = lax.broadcasted_iota(jnp.int32, (rows, 2 * ROPE), 1) % ROPE
    position = (lax.broadcasted_iota(jnp.int32, (rows, 2 * ROPE), 0) + c * rows).astype(jnp.float32)
    angles = position * freq_ref[0:1, :]
    low = lane < ROPE // 2
    cosine = jnp.cos(angles)
    sine = jnp.sin(angles)
    sine = jnp.where(low, -sine, sine)

    loads[5].wait()
    seg_now = seg_ref[pl.ds(c, 1), :].astype(jnp.float32)
    query_seg = jnp.transpose(jnp.broadcast_to(seg_now, (rows, rows)))
    row_id = lax.broadcasted_iota(jnp.int32, (rows, rows), 0)
    col_id = lax.broadcasted_iota(jnp.int32, (rows, rows), 1)

    def mask_of(j):
        key_seg = seg_ref[pl.ds(lax.rem(c - j + n, n), 1), :].astype(jnp.float32)
        same = query_seg == jnp.broadcast_to(key_seg, (rows, rows))
        if j == 0:
            return same & (col_id <= row_id)
        valid = jnp.broadcast_to(c, (rows, rows)) >= j
        return same & valid

    loads[0].wait()
    loads[4].wait()
    before_tri = (row_id < col_id).astype(jnp.bfloat16)

    def ranks(named):
        rank = jnp.dot(
            named.astype(jnp.bfloat16), before_tri, preferred_element_type=jnp.float32
        )
        return jnp.where(named, rank, -1.0)

    def pick(picker, block):
        return lax.dot_general(
            picker.astype(jnp.bfloat16), block, (((1,), (1,)), ((), ())),
            preferred_element_type=jnp.float32,
        ).astype(jnp.bfloat16)

    line = lax.broadcasted_iota(jnp.int32, (n * slots, rows), 0)
    wanted = lax.rem(c + line // slots, n) * cores + d
    named = jnp.broadcast_to(owners[last], (n * slots, rows)) == wanted
    picked = pick(ranks(named) == (line % slots).astype(jnp.float32), held[last])
    kv_ref[0, c] = picked[:slots]
    for j in range(1, n):
        compact[j] = picked[j * slots:(j + 1) * slots]

    loads[1].wait()
    loads[2].wait()
    pair_width = 2 * (NOPE + ROPE)

    @pl.loop(0, heads // 2)
    def _(p):
        qp = qv[:, pl.ds(pl.multiple_of(p * pair_width, 128), pair_width)]
        rope = jnp.concatenate(
            [qp[:, NOPE:NOPE + ROPE], qp[:, 2 * NOPE + ROPE:]], axis=1
        ).astype(jnp.float32)
        swapped = jnp.where(
            low,
            pltpu.roll(rope, 2 * ROPE - ROPE // 2, 1),
            pltpu.roll(rope, ROPE // 2, 1),
        )
        rotated = (rope * cosine + swapped * sine).astype(jnp.bfloat16)
        qf[2 * p, :, LATENT:] = rotated[:, :ROPE]
        qf[2 * p + 1, :, LATENT:] = rotated[:, ROPE:]
        for k, start in ((0, 0), (1, NOPE + ROPE)):
            qf[2 * p + k, :, :LATENT] = jnp.dot(
                qp[:, start:start + NOPE], ak[2 * p + k], preferred_element_type=jnp.float32
            ).astype(jnp.bfloat16)

    for j in range(1, n):
        if j > back:
            ksends[j].start()
        else:
            @pl.when(c + j >= n)
            def _():
                ksends[j].start()
    if back:
        forward(1)
    size = chunk * rows
    own_mask = mask_of(0)

    def scores_of(i, keys, mask):
        q = qf[pl.ds(i * chunk, chunk)].reshape(size, LATENT + ROPE)
        s = jnp.dot(q, keys, preferred_element_type=jnp.float32)
        s = s.reshape(chunk, rows, keys.shape[1]) * scale
        return jnp.where(mask[None], s, NEG).reshape(size, keys.shape[1])

    def spread(j, at):
        values[at:at + rows] = jnp.transpose(held[last - j, :LATENT])

    def finish(i, total, sums):
        latent = (total / sums).astype(jnp.bfloat16)
        for k in range(chunk):
            h = i * chunk + k
            out_ref[:, pl.ds(pl.multiple_of(h * VDIM, VDIM), VDIM)] = jnp.dot(
                latent[k * rows:(k + 1) * rows], av[h], preferred_element_type=jnp.float32
            ).astype(jnp.bfloat16)

    spread(0, 0)

    @pl.loop(0, heads // chunk)
    def _(i):
        keys = held[last]
        s = scores_of(i, keys, own_mask)
        top = jnp.max(s, axis=1, keepdims=True)
        e = jnp.exp(s - top)
        at = pl.ds(pl.multiple_of(i * size, size), size)
        m_ref[at] = top
        l_ref[at] = jnp.sum(e, axis=1, keepdims=True)
        acc[at] = jnp.dot(
            e.astype(jnp.bfloat16), values[:rows], preferred_element_type=jnp.float32
        )

    groups = [list(range(j, min(j + 2, back + 1))) for j in range(1, back + 1, 2)]

    def settle(j):
        @pl.when(c >= j)
        def _():
            for k in range(1, cores):
                forwards[j, k].wait_recv()

    loads[3].wait()
    for g, group in enumerate(groups):
        for j in group:
            if j > 1:
                forward(j)
        for j in group:
            settle(j)
        mask = jnp.concatenate([mask_of(j) for j in reversed(group)], axis=1)
        for at, j in enumerate(reversed(group)):
            spread(j, at * rows)
        final = g == len(groups) - 1

        def step(i):
            keys = jnp.concatenate([held[last - j] for j in reversed(group)], axis=1)
            s = scores_of(i, keys, mask)
            at = pl.ds(pl.multiple_of(i * size, size), size)
            before = m_ref[at]
            top = jnp.maximum(before, jnp.max(s, axis=1, keepdims=True))
            e = jnp.exp(s - top)
            shrink = jnp.exp(before - top)
            sums = l_ref[at] * shrink + jnp.sum(e, axis=1, keepdims=True)
            total = acc[at] * shrink + jnp.dot(
                e.astype(jnp.bfloat16), values[:len(group) * rows],
                preferred_element_type=jnp.float32,
            )
            if final:
                finish(i, total, sums)
            else:
                m_ref[at] = top
                l_ref[at] = sums
                acc[at] = total

        pl.loop(0, heads // chunk)(step)

    me = c * cores + d
    slot_id = lax.broadcasted_iota(jnp.int32, (slots, rows), 0).astype(jnp.float32)
    for j in range(1, n):
        if j > back:
            ksends[j].wait()
            continue

        @pl.when(c + j >= n)
        def _():
            ksends[j].wait_send()

        @pl.when(c < j)
        def _():
            ksends[j].wait_recv()

        @pl.when(c + j < n)
        def _():
            sends[j].wait_send()
            osends[j].wait_send()

        @pl.when(c >= j)
        def _():
            osends[j].wait_recv()
            named = jnp.broadcast_to(owners[last - j], (8, rows)) == me
            rank = jnp.broadcast_to(ranks(named)[0:1], (slots, rows))
            kv_ref[0, c - j] = pick(rank == slot_id, held[last - j])
            for k in range(1, cores):
                forwards[j, k].wait_send()


def passing(pieces, *refs):
    count = len(refs) // 3
    sources, targets, held, (sem,) = (
        refs[:count], refs[count:2 * count], refs[2 * count:3 * count], refs[3 * count:]
    )
    loads, stores = [], []
    for i, (source, target, room) in enumerate(zip(sources, targets, held)):
        step = source.shape[0] // pieces[i]
        for k in range(pieces[i]):
            at = pl.ds(k * step, step)
            spot = len(loads)
            loads.append(pltpu.make_async_copy(source.at[at], room.at[at], sem.at[0, spot]))
            stores.append(pltpu.make_async_copy(room.at[at], target.at[at], sem.at[1, spot]))
    for load in loads:
        load.start()
    for load, store in zip(loads, stores):
        load.wait()
        store.start()
    for store in stores:
        store.wait()


def hand_over(*arrays):
    pieces = (4, 1)
    hbm = pl.BlockSpec(memory_space=pltpu.HBM)
    return pl.pallas_call(
        functools.partial(passing, pieces),
        out_shape=tuple(jax.ShapeDtypeStruct(a.shape, a.dtype) for a in arrays),
        in_specs=[hbm] * len(arrays),
        out_specs=(hbm,) * len(arrays),
        scratch_shapes=[pltpu.VMEM(a.shape, a.dtype) for a in arrays]
        + [pltpu.SemaphoreType.DMA((2, sum(pieces)))],
        compiler_params=pltpu.CompilerParams(vmem_limit_bytes=66200000),
    )(*arrays)


def on_device(sizes, queries, latent_rows, segments, owners, absorb_key, absorb_value):
    n, cores = sizes
    rows = latent_rows.shape[0]
    width = LATENT + ROPE
    heads = absorb_key.shape[0]
    tokens = segments.shape[0]
    back = min(n - 1, cdiv(tokens // 2 - 1, rows))
    slots = max(2, 2 * rows // (n * cores))
    chunk = 4
    frequency = 10000.0 ** (-np.arange(ROPE // 2, dtype=np.float32) * 2.0 / ROPE)
    frequency = np.tile(frequency.astype(np.float32), 4)[None, :]
    segment_rows = segments.reshape(n, rows)
    owner_rows = owners.reshape(1, rows)
    vmem = pl.BlockSpec(memory_space=pltpu.VMEM)
    hbm = pl.BlockSpec(memory_space=pltpu.HBM)
    dma = pltpu.SemaphoreType.DMA
    results = pl.pallas_call(
        functools.partial(kernel, n, cores, back, slots, chunk),
        out_shape=(
            jax.ShapeDtypeStruct((rows, heads * VDIM), jnp.bfloat16),
            jax.ShapeDtypeStruct((1, n, slots, width), jnp.bfloat16),
        ),
        in_specs=[vmem, hbm, hbm, hbm, hbm, hbm, hbm],
        out_specs=(vmem, vmem),
        scratch_shapes=[
            pltpu.VMEM(queries.shape, jnp.bfloat16),
            pltpu.VMEM(absorb_key.shape, jnp.bfloat16),
            pltpu.VMEM(absorb_value.shape, jnp.bfloat16),
            pltpu.VMEM((heads, rows, width), jnp.bfloat16),
            pltpu.VMEM((heads * rows, LATENT), jnp.float32),
            pltpu.VMEM((heads * rows, 1), jnp.float32),
            pltpu.VMEM((heads * rows, 1), jnp.float32),
            pltpu.VMEM((n, width, rows), jnp.bfloat16),
            pltpu.VMEM((2 * rows, LATENT), jnp.bfloat16),
            pltpu.VMEM((n, 1, rows), jnp.int32),
            pltpu.VMEM((n, rows), jnp.int32),
            pltpu.VMEM((n, slots, width), jnp.bfloat16),
            dma((6,)),
            dma((n,)),
            dma((n,)),
            dma((n, cores)),
            dma((n, cores)),
            dma((n,)),
            dma((n,)),
            dma((n,)),
            dma((n,)),
        ],
        compiler_params=pltpu.CompilerParams(
            collective_id=0, has_side_effects=True, vmem_limit_bytes=66200000
        ),
    )(frequency, segment_rows, owner_rows, latent_rows.T, queries, absorb_key, absorb_value)
    return tuple(hand_over(*results))


def solution(mesh):
    in_specs = (
        P(("group", "ctx"), ("head", "dec")),
        P(("group", "ctx"), None),
        P("group"),
        P(("group", "ctx"), None),
        P(("head", "dec"), None, None),
        P(("head", "dec"), None, None),
    )
    out_specs = (P(("group", "ctx"), ("head", "dec")), P(("group", "ctx", "dec"), None, None, None))
    sizes = (mesh.shape["ctx"], mesh.shape["dec"])
    return jax.shard_map(
        functools.partial(on_device, sizes),
        mesh=mesh, in_specs=in_specs, out_specs=out_specs, check_vma=False,
    )
```

```python
import functools

import jax
import jax.numpy as jnp
import numpy as np
from jax import lax
from jax.experimental import pallas as pl
from jax.experimental.pallas import tpu as pltpu
from jax.sharding import PartitionSpec as P

NOPE = 128
ROPE = 64
LATENT = 512
VDIM = 128
MESH = pl.DeviceIdType.MESH
NEG = -1e30


def cdiv(a, b):
    return -(-a // b)


def kernel(
    n, cores, back, slots, chunk,
    freq_ref, seg_hbm, owners_hbm, rows_hbm, q_hbm, ak_hbm, av_hbm,
    out_ref, kv_ref,
    qv, ak, av, qf, acc, m_ref, l_ref, held, values, owners, seg_ref, compact,
    local_sem, send_sem, recv_sem, fsend_sem, frecv_sem, osend_sem, orecv_sem,
    ksend_sem, krecv_sem,
):
    c = lax.axis_index("ctx")
    d = lax.axis_index("dec")
    rows = rows_hbm.shape[1]
    heads = ak_hbm.shape[0]
    part = (LATENT + ROPE) // cores
    scale = (NOPE + ROPE) ** (-0.5)
    last = n - 1

    loads = [
        pltpu.make_async_copy(rows_hbm, held.at[last], local_sem.at[0]),
        pltpu.make_async_copy(q_hbm, qv, local_sem.at[1]),
        pltpu.make_async_copy(ak_hbm, ak, local_sem.at[2]),
        pltpu.make_async_copy(av_hbm, av, local_sem.at[3]),
        pltpu.make_async_copy(owners_hbm, owners.at[last], local_sem.at[4]),
        pltpu.make_async_copy(seg_hbm, seg_ref, local_sem.at[5]),
    ]
    for load in loads:
        load.start()

    barrier = pltpu.get_barrier_semaphore()
    for j in range(1, n):
        pl.semaphore_signal(
            barrier, inc=1, device_id={"ctx": lax.rem(c + j, n)}, device_id_type=MESH
        )
    for k in range(1, cores):
        pl.semaphore_signal(
            barrier, inc=1, device_id={"dec": lax.rem(d + k, cores)}, device_id_type=MESH
        )
    pl.semaphore_wait(barrier, n - 1 + cores - 1)

    mine = pl.ds(pl.multiple_of(d * part, part), part)
    sends, osends, ksends = {}, {}, {}
    for j in range(1, n):
        target = {"ctx": lax.rem(c + j, n)}
        ksends[j] = pltpu.make_async_remote_copy(
            src_ref=compact.at[j],
            dst_ref=kv_ref.at[0, c],
            send_sem=ksend_sem.at[j],
            recv_sem=krecv_sem.at[j],
            device_id=target,
            device_id_type=MESH,
        )
        if j > back:
            continue
        sends[j] = pltpu.make_async_remote_copy(
            src_ref=rows_hbm.at[mine],
            dst_ref=held.at[last - j, mine],
            send_sem=send_sem.at[j],
            recv_sem=recv_sem.at[j],
            device_id=target,
            device_id_type=MESH,
        )
        osends[j] = pltpu.make_async_remote_copy(
            src_ref=owners_hbm,
            dst_ref=owners.at[last - j],
            send_sem=osend_sem.at[j],
            recv_sem=orecv_sem.at[j],
            device_id=target,
            device_id_type=MESH,
        )

    for j in sends:
        @pl.when(c + j < n)
        def _():
            sends[j].start()
    for j in sends:
        @pl.when(c + j < n)
        def _():
            osends[j].start()

        @pl.when(c < j)
        def _():
            held[last - j] = jnp.zeros_like(held[last - j])

    forwards = {}
    for j in sends:
        for k in range(1, cores):
            forwards[j, k] = pltpu.make_async_remote_copy(
                src_ref=held.at[last - j, mine],
                dst_ref=held.at[last - j, mine],
                send_sem=fsend_sem.at[j, k],
                recv_sem=frecv_sem.at[j, k],
                device_id={"dec": lax.rem(d + k, cores)},
                device_id_type=MESH,
            )

    def forward(j):
        @pl.when(c >= j)
        def _():
            sends[j].wait_recv()
            for k in range(1, cores):
                forwards[j, k].start()

    lane = lax.broadcasted_iota(jnp.int32, (rows, 2 * ROPE), 1) % ROPE
    position = (lax.broadcasted_iota(jnp.int32, (rows, 2 * ROPE), 0) + c * rows).astype(jnp.float32)
    angles = position * freq_ref[0:1, :]
    low = lane < ROPE // 2
    cosine = jnp.cos(angles)
    sine = jnp.sin(angles)
    sine = jnp.where(low, -sine, sine)

    loads[5].wait()
    seg_now = seg_ref[pl.ds(c, 1), :].astype(jnp.float32)
    query_seg = jnp.transpose(jnp.broadcast_to(seg_now, (rows, rows)))
    row_id = lax.broadcasted_iota(jnp.int32, (rows, rows), 0)
    col_id = lax.broadcasted_iota(jnp.int32, (rows, rows), 1)

    def mask_of(j):
        key_seg = seg_ref[pl.ds(lax.rem(c - j + n, n), 1), :].astype(jnp.float32)
        same = query_seg == jnp.broadcast_to(key_seg, (rows, rows))
        if j == 0:
            return same & (col_id <= row_id)
        valid = jnp.broadcast_to(c, (rows, rows)) >= j
        return same & valid

    loads[0].wait()
    loads[4].wait()
    before_tri = (row_id < col_id).astype(jnp.bfloat16)

    def ranks(named):
        rank = jnp.dot(
            named.astype(jnp.bfloat16), before_tri, preferred_element_type=jnp.float32
        )
        return jnp.where(named, rank, -1.0)

    def pick(picker, block):
        return lax.dot_general(
            picker.astype(jnp.bfloat16), block, (((1,), (1,)), ((), ())),
            preferred_element_type=jnp.float32,
        ).astype(jnp.bfloat16)

    line = lax.broadcasted_iota(jnp.int32, (n * slots, rows), 0)
    wanted = lax.rem(c + line // slots, n) * cores + d
    named = jnp.broadcast_to(owners[last], (n * slots, rows)) == wanted
    picked = pick(ranks(named) == (line % slots).astype(jnp.float32), held[last])
    kv_ref[0, c] = picked[:slots]
    for j in range(1, n):
        compact[j] = picked[j * slots:(j + 1) * slots]

    loads[1].wait()
    loads[2].wait()
    pair_width = 2 * (NOPE + ROPE)

    @pl.loop(0, heads // 2)
    def _(p):
        qp = qv[:, pl.ds(pl.multiple_of(p * pair_width, 128), pair_width)]
        rope = jnp.concatenate(
            [qp[:, NOPE:NOPE + ROPE], qp[:, 2 * NOPE + ROPE:]], axis=1
        ).astype(jnp.float32)
        swapped = jnp.where(
            low,
            pltpu.roll(rope, 2 * ROPE - ROPE // 2, 1),
            pltpu.roll(rope, ROPE // 2, 1),
        )
        rotated = (rope * cosine + swapped * sine).astype(jnp.bfloat16)
        qf[2 * p, :, LATENT:] = rotated[:, :ROPE]
        qf[2 * p + 1, :, LATENT:] = rotated[:, ROPE:]
        for k, start in ((0, 0), (1, NOPE + ROPE)):
            qf[2 * p + k, :, :LATENT] = jnp.dot(
                qp[:, start:start + NOPE], ak[2 * p + k], preferred_element_type=jnp.float32
            ).astype(jnp.bfloat16)

    for j in range(1, n):
        if j > back:
            ksends[j].start()
        else:
            @pl.when(c + j >= n)
            def _():
                ksends[j].start()
    if back:
        forward(1)
    size = chunk * rows
    own_mask = mask_of(0)

    def scores_of(i, keys, mask):
        q = qf[pl.ds(i * chunk, chunk)].reshape(size, LATENT + ROPE)
        s = jnp.dot(q, keys, preferred_element_type=jnp.float32)
        s = s.reshape(chunk, rows, keys.shape[1]) * scale
        return jnp.where(mask[None], s, NEG).reshape(size, keys.shape[1])

    def spread(j, at):
        values[at:at + rows] = jnp.transpose(held[last - j, :LATENT])

    def finish(i, total, sums):
        latent = (total / sums).astype(jnp.bfloat16)
        for k in range(chunk):
            h = i * chunk + k
            out_ref[:, pl.ds(pl.multiple_of(h * VDIM, VDIM), VDIM)] = jnp.dot(
                latent[k * rows:(k + 1) * rows], av[h], preferred_element_type=jnp.float32
            ).astype(jnp.bfloat16)

    spread(0, 0)

    @pl.loop(0, heads // chunk)
    def _(i):
        keys = held[last]
        s = scores_of(i, keys, own_mask)
        top = jnp.max(s, axis=1, keepdims=True)
        e = jnp.exp(s - top)
        at = pl.ds(pl.multiple_of(i * size, size), size)
        m_ref[at] = top
        l_ref[at] = jnp.sum(e, axis=1, keepdims=True)
        acc[at] = jnp.dot(
            e.astype(jnp.bfloat16), values[:rows], preferred_element_type=jnp.float32
        )

    groups = [list(range(j, min(j + 2, back + 1))) for j in range(1, back + 1, 2)]

    def settle(j):
        @pl.when(c >= j)
        def _():
            for k in range(1, cores):
                forwards[j, k].wait_recv()

    loads[3].wait()
    for g, group in enumerate(groups):
        for j in group:
            if j > 1:
                forward(j)
        for j in group:
            settle(j)
        mask = jnp.concatenate([mask_of(j) for j in reversed(group)], axis=1)
        for at, j in enumerate(reversed(group)):
            spread(j, at * rows)
        final = g == len(groups) - 1

        def step(i):
            keys = jnp.concatenate([held[last - j] for j in reversed(group)], axis=1)
            s = scores_of(i, keys, mask)
            at = pl.ds(pl.multiple_of(i * size, size), size)
            before = m_ref[at]
            top = jnp.maximum(before, jnp.max(s, axis=1, keepdims=True))
            e = jnp.exp(s - top)
            shrink = jnp.exp(before - top)
            sums = l_ref[at] * shrink + jnp.sum(e, axis=1, keepdims=True)
            total = acc[at] * shrink + jnp.dot(
                e.astype(jnp.bfloat16), values[:len(group) * rows],
                preferred_element_type=jnp.float32,
            )
            if final:
                finish(i, total, sums)
            else:
                m_ref[at] = top
                l_ref[at] = sums
                acc[at] = total

        pl.loop(0, heads // chunk)(step)

    me = c * cores + d
    slot_id = lax.broadcasted_iota(jnp.int32, (slots, rows), 0).astype(jnp.float32)
    for j in range(1, n):
        if j > back:
            ksends[j].wait()
            continue

        @pl.when(c + j >= n)
        def _():
            ksends[j].wait_send()

        @pl.when(c < j)
        def _():
            ksends[j].wait_recv()

        @pl.when(c + j < n)
        def _():
            sends[j].wait_send()
            osends[j].wait_send()

        @pl.when(c >= j)
        def _():
            osends[j].wait_recv()
            named = jnp.broadcast_to(owners[last - j], (8, rows)) == me
            rank = jnp.broadcast_to(ranks(named)[0:1], (slots, rows))
            kv_ref[0, c - j] = pick(rank == slot_id, held[last - j])
            for k in range(1, cores):
                forwards[j, k].wait_send()


def passing(pieces, *refs):
    count = len(refs) // 3
    sources, targets, held, (sem,) = (
        refs[:count], refs[count:2 * count], refs[2 * count:3 * count], refs[3 * count:]
    )
    loads, stores = [], []
    for i, (source, target, room) in enumerate(zip(sources, targets, held)):
        step = source.shape[0] // pieces[i]
        for k in range(pieces[i]):
            at = pl.ds(k * step, step)
            spot = len(loads)
            loads.append(pltpu.make_async_copy(source.at[at], room.at[at], sem.at[0, spot]))
            stores.append(pltpu.make_async_copy(room.at[at], target.at[at], sem.at[1, spot]))
    for load in loads:
        load.start()
    for load, store in zip(loads, stores):
        load.wait()
        store.start()
    for store in stores:
        store.wait()


def hand_over(*arrays):
    pieces = (4, 1)
    hbm = pl.BlockSpec(memory_space=pltpu.HBM)
    return pl.pallas_call(
        functools.partial(passing, pieces),
        out_shape=tuple(jax.ShapeDtypeStruct(a.shape, a.dtype) for a in arrays),
        in_specs=[hbm] * len(arrays),
        out_specs=(hbm,) * len(arrays),
        scratch_shapes=[pltpu.VMEM(a.shape, a.dtype) for a in arrays]
        + [pltpu.SemaphoreType.DMA((2, sum(pieces)))],
        compiler_params=pltpu.CompilerParams(vmem_limit_bytes=66200000),
    )(*arrays)


def on_device(sizes, queries, latent_rows, segments, owners, absorb_key, absorb_value):
    n, cores = sizes
    rows = latent_rows.shape[0]
    width = LATENT + ROPE
    heads = absorb_key.shape[0]
    tokens = segments.shape[0]
    back = min(n - 1, cdiv(tokens // 2 - 1, rows))
    slots = max(2, 2 * rows // (n * cores))
    chunk = heads
    frequency = 10000.0 ** (-np.arange(ROPE // 2, dtype=np.float32) * 2.0 / ROPE)
    frequency = np.tile(frequency.astype(np.float32), 4)[None, :]
    segment_rows = segments.reshape(n, rows)
    owner_rows = owners.reshape(1, rows)
    vmem = pl.BlockSpec(memory_space=pltpu.VMEM)
    hbm = pl.BlockSpec(memory_space=pltpu.HBM)
    dma = pltpu.SemaphoreType.DMA
    results = pl.pallas_call(
        functools.partial(kernel, n, cores, back, slots, chunk),
        out_shape=(
            jax.ShapeDtypeStruct((rows, heads * VDIM), jnp.bfloat16),
            jax.ShapeDtypeStruct((1, n, slots, width), jnp.bfloat16),
        ),
        in_specs=[vmem, hbm, hbm, hbm, hbm, hbm, hbm],
        out_specs=(vmem, vmem),
        scratch_shapes=[
            pltpu.VMEM(queries.shape, jnp.bfloat16),
            pltpu.VMEM(absorb_key.shape, jnp.bfloat16),
            pltpu.VMEM(absorb_value.shape, jnp.bfloat16),
            pltpu.VMEM((heads, rows, width), jnp.bfloat16),
            pltpu.VMEM((heads * rows, LATENT), jnp.float32),
            pltpu.VMEM((heads * rows, 1), jnp.float32),
            pltpu.VMEM((heads * rows, 1), jnp.float32),
            pltpu.VMEM((n, width, rows), jnp.bfloat16),
            pltpu.VMEM((2 * rows, LATENT), jnp.bfloat16),
            pltpu.VMEM((n, 1, rows), jnp.int32),
            pltpu.VMEM((n, rows), jnp.int32),
            pltpu.VMEM((n, slots, width), jnp.bfloat16),
            dma((6,)),
            dma((n,)),
            dma((n,)),
            dma((n, cores)),
            dma((n, cores)),
            dma((n,)),
            dma((n,)),
            dma((n,)),
            dma((n,)),
        ],
        compiler_params=pltpu.CompilerParams(
            collective_id=0, has_side_effects=True, vmem_limit_bytes=66200000
        ),
    )(frequency, segment_rows, owner_rows, latent_rows.T, queries, absorb_key, absorb_value)
    return tuple(hand_over(*results))


def solution(mesh):
    in_specs = (
        P(("group", "ctx"), ("head", "dec")),
        P(("group", "ctx"), None),
        P("group"),
        P(("group", "ctx"), None),
        P(("head", "dec"), None, None),
        P(("head", "dec"), None, None),
    )
    out_specs = (P(("group", "ctx"), ("head", "dec")), P(("group", "ctx", "dec"), None, None, None))
    sizes = (mesh.shape["ctx"], mesh.shape["dec"])
    return jax.shard_map(
        functools.partial(on_device, sizes),
        mesh=mesh, in_specs=in_specs, out_specs=out_specs, check_vma=False,
    )
```

```python
import functools

import jax
import jax.numpy as jnp
import numpy as np
from jax import lax
from jax.experimental import pallas as pl
from jax.experimental.pallas import tpu as pltpu
from jax.sharding import PartitionSpec as P

NOPE = 128
ROPE = 64
LATENT = 512
VDIM = 128
MESH = pl.DeviceIdType.MESH
NEG = -1e30


def cdiv(a, b):
    return -(-a // b)


def kernel(
    n, cores, back, slots, chunk,
    freq_ref, seg_hbm, owners_hbm, rows_hbm, q_hbm, ak_hbm, av_hbm,
    out_ref, kv_ref,
    qv, ak, av, qf, acc, m_ref, l_ref, held, values, owners, seg_ref, compact,
    local_sem, send_sem, recv_sem, fsend_sem, frecv_sem, osend_sem, orecv_sem,
    ksend_sem, krecv_sem,
):
    c = lax.axis_index("ctx")
    d = lax.axis_index("dec")
    rows = rows_hbm.shape[1]
    heads = ak_hbm.shape[0]
    part = (LATENT + ROPE) // cores
    scale = (NOPE + ROPE) ** (-0.5)
    last = n - 1

    loads = [
        pltpu.make_async_copy(rows_hbm, held.at[last], local_sem.at[0]),
        pltpu.make_async_copy(q_hbm, qv, local_sem.at[1]),
        pltpu.make_async_copy(ak_hbm, ak, local_sem.at[2]),
        pltpu.make_async_copy(av_hbm, av, local_sem.at[3]),
        pltpu.make_async_copy(owners_hbm, owners.at[last], local_sem.at[4]),
        pltpu.make_async_copy(seg_hbm, seg_ref, local_sem.at[5]),
    ]
    for load in loads:
        load.start()

    barrier = pltpu.get_barrier_semaphore()
    for j in range(1, n):
        pl.semaphore_signal(
            barrier, inc=1, device_id={"ctx": lax.rem(c + j, n)}, device_id_type=MESH
        )
    for k in range(1, cores):
        pl.semaphore_signal(
            barrier, inc=1, device_id={"dec": lax.rem(d + k, cores)}, device_id_type=MESH
        )
    pl.semaphore_wait(barrier, n - 1 + cores - 1)

    mine = pl.ds(pl.multiple_of(d * part, part), part)
    sends, osends, ksends = {}, {}, {}
    for j in range(1, n):
        target = {"ctx": lax.rem(c + j, n)}
        ksends[j] = pltpu.make_async_remote_copy(
            src_ref=compact.at[j],
            dst_ref=kv_ref.at[0, c],
            send_sem=ksend_sem.at[j],
            recv_sem=krecv_sem.at[j],
            device_id=target,
            device_id_type=MESH,
        )
        if j > back:
            continue
        sends[j] = pltpu.make_async_remote_copy(
            src_ref=rows_hbm.at[mine],
            dst_ref=held.at[last - j, mine],
            send_sem=send_sem.at[j],
            recv_sem=recv_sem.at[j],
            device_id=target,
            device_id_type=MESH,
        )
        osends[j] = pltpu.make_async_remote_copy(
            src_ref=owners_hbm,
            dst_ref=owners.at[last - j],
            send_sem=osend_sem.at[j],
            recv_sem=orecv_sem.at[j],
            device_id=target,
            device_id_type=MESH,
        )

    for j in sends:
        @pl.when(c + j < n)
        def _():
            sends[j].start()
    for j in sends:
        @pl.when(c + j < n)
        def _():
            osends[j].start()

        @pl.when(c < j)
        def _():
            held[last - j] = jnp.zeros_like(held[last - j])

    forwards = {}
    for j in sends:
        for k in range(1, cores):
            forwards[j, k] = pltpu.make_async_remote_copy(
                src_ref=held.at[last - j, mine],
                dst_ref=held.at[last - j, mine],
                send_sem=fsend_sem.at[j, k],
                recv_sem=frecv_sem.at[j, k],
                device_id={"dec": lax.rem(d + k, cores)},
                device_id_type=MESH,
            )

    def forward(j):
        @pl.when(c >= j)
        def _():
            sends[j].wait_recv()
            for k in range(1, cores):
                forwards[j, k].start()

    lane = lax.broadcasted_iota(jnp.int32, (rows, 2 * ROPE), 1) % ROPE
    position = (lax.broadcasted_iota(jnp.int32, (rows, 2 * ROPE), 0) + c * rows).astype(jnp.float32)
    angles = position * freq_ref[0:1, :]
    low = lane < ROPE // 2
    cosine = jnp.cos(angles)
    sine = jnp.sin(angles)
    sine = jnp.where(low, -sine, sine)

    loads[5].wait()
    seg_now = seg_ref[pl.ds(c, 1), :].astype(jnp.float32)
    query_seg = jnp.transpose(jnp.broadcast_to(seg_now, (rows, rows)))
    row_id = lax.broadcasted_iota(jnp.int32, (rows, rows), 0)
    col_id = lax.broadcasted_iota(jnp.int32, (rows, rows), 1)

    def mask_of(j):
        key_seg = seg_ref[pl.ds(lax.rem(c - j + n, n), 1), :].astype(jnp.float32)
        same = query_seg == jnp.broadcast_to(key_seg, (rows, rows))
        if j == 0:
            return same & (col_id <= row_id)
        valid = jnp.broadcast_to(c, (rows, rows)) >= j
        return same & valid

    loads[0].wait()
    loads[4].wait()
    before_tri = (row_id < col_id).astype(jnp.bfloat16)

    def ranks(named):
        rank = jnp.dot(
            named.astype(jnp.bfloat16), before_tri, preferred_element_type=jnp.float32
        )
        return jnp.where(named, rank, -1.0)

    def pick(picker, block):
        return lax.dot_general(
            picker.astype(jnp.bfloat16), block, (((1,), (1,)), ((), ())),
            preferred_element_type=jnp.float32,
        ).astype(jnp.bfloat16)

    line = lax.broadcasted_iota(jnp.int32, (n * slots, rows), 0)
    wanted = lax.rem(c + line // slots, n) * cores + d
    named = jnp.broadcast_to(owners[last], (n * slots, rows)) == wanted
    picked = pick(ranks(named) == (line % slots).astype(jnp.float32), held[last])
    kv_ref[0, c] = picked[:slots]
    for j in range(1, n):
        compact[j] = picked[j * slots:(j + 1) * slots]

    loads[1].wait()
    loads[2].wait()
    pair_width = 2 * (NOPE + ROPE)

    @pl.loop(0, heads // 2, unroll=2)
    def _(p):
        qp = qv[:, pl.ds(pl.multiple_of(p * pair_width, 128), pair_width)]
        rope = jnp.concatenate(
            [qp[:, NOPE:NOPE + ROPE], qp[:, 2 * NOPE + ROPE:]], axis=1
        ).astype(jnp.float32)
        swapped = jnp.where(
            low,
            pltpu.roll(rope, 2 * ROPE - ROPE // 2, 1),
            pltpu.roll(rope, ROPE // 2, 1),
        )
        rotated = (rope * cosine + swapped * sine).astype(jnp.bfloat16)
        qf[2 * p, :, LATENT:] = rotated[:, :ROPE]
        qf[2 * p + 1, :, LATENT:] = rotated[:, ROPE:]
        for k, start in ((0, 0), (1, NOPE + ROPE)):
            qf[2 * p + k, :, :LATENT] = jnp.dot(
                qp[:, start:start + NOPE], ak[2 * p + k], preferred_element_type=jnp.float32
            ).astype(jnp.bfloat16)

    for j in range(1, n):
        if j > back:
            ksends[j].start()
        else:
            @pl.when(c + j >= n)
            def _():
                ksends[j].start()
    if back:
        forward(1)
    size = chunk * rows
    own_mask = mask_of(0)

    def scores_of(i, keys, mask):
        q = qf[pl.ds(i * chunk, chunk)].reshape(size, LATENT + ROPE)
        s = jnp.dot(q, keys, preferred_element_type=jnp.float32)
        s = s.reshape(chunk, rows, keys.shape[1]) * scale
        return jnp.where(mask[None], s, NEG).reshape(size, keys.shape[1])

    def spread(j, at):
        values[at:at + rows] = jnp.transpose(held[last - j, :LATENT])

    def finish(i, total, sums):
        latent = (total / sums).astype(jnp.bfloat16)
        for k in range(chunk):
            h = i * chunk + k
            out_ref[:, pl.ds(pl.multiple_of(h * VDIM, VDIM), VDIM)] = jnp.dot(
                latent[k * rows:(k + 1) * rows], av[h], preferred_element_type=jnp.float32
            ).astype(jnp.bfloat16)

    spread(0, 0)

    @pl.loop(0, heads // chunk)
    def _(i):
        keys = held[last]
        s = scores_of(i, keys, own_mask)
        top = jnp.max(s, axis=1, keepdims=True)
        e = jnp.exp(s - top)
        at = pl.ds(pl.multiple_of(i * size, size), size)
        m_ref[at] = top
        l_ref[at] = jnp.sum(e, axis=1, keepdims=True)
        acc[at] = jnp.dot(
            e.astype(jnp.bfloat16), values[:rows], preferred_element_type=jnp.float32
        )

    groups = [list(range(j, min(j + 2, back + 1))) for j in range(1, back + 1, 2)]

    def settle(j):
        @pl.when(c >= j)
        def _():
            for k in range(1, cores):
                forwards[j, k].wait_recv()

    loads[3].wait()
    for g, group in enumerate(groups):
        for j in group:
            if j > 1:
                forward(j)
        for j in group:
            settle(j)
        mask = jnp.concatenate([mask_of(j) for j in reversed(group)], axis=1)
        for at, j in enumerate(reversed(group)):
            spread(j, at * rows)
        final = g == len(groups) - 1

        def step(i):
            keys = jnp.concatenate([held[last - j] for j in reversed(group)], axis=1)
            s = scores_of(i, keys, mask)
            at = pl.ds(pl.multiple_of(i * size, size), size)
            before = m_ref[at]
            top = jnp.maximum(before, jnp.max(s, axis=1, keepdims=True))
            e = jnp.exp(s - top)
            shrink = jnp.exp(before - top)
            sums = l_ref[at] * shrink + jnp.sum(e, axis=1, keepdims=True)
            total = acc[at] * shrink + jnp.dot(
                e.astype(jnp.bfloat16), values[:len(group) * rows],
                preferred_element_type=jnp.float32,
            )
            if final:
                finish(i, total, sums)
            else:
                m_ref[at] = top
                l_ref[at] = sums
                acc[at] = total

        pl.loop(0, heads // chunk)(step)

    me = c * cores + d
    slot_id = lax.broadcasted_iota(jnp.int32, (slots, rows), 0).astype(jnp.float32)
    for j in range(1, n):
        if j > back:
            ksends[j].wait()
            continue

        @pl.when(c + j >= n)
        def _():
            ksends[j].wait_send()

        @pl.when(c < j)
        def _():
            ksends[j].wait_recv()

        @pl.when(c + j < n)
        def _():
            sends[j].wait_send()
            osends[j].wait_send()

        @pl.when(c >= j)
        def _():
            osends[j].wait_recv()
            named = jnp.broadcast_to(owners[last - j], (8, rows)) == me
            rank = jnp.broadcast_to(ranks(named)[0:1], (slots, rows))
            kv_ref[0, c - j] = pick(rank == slot_id, held[last - j])
            for k in range(1, cores):
                forwards[j, k].wait_send()


def passing(pieces, *refs):
    count = len(refs) // 3
    sources, targets, held, (sem,) = (
        refs[:count], refs[count:2 * count], refs[2 * count:3 * count], refs[3 * count:]
    )
    loads, stores = [], []
    for i, (source, target, room) in enumerate(zip(sources, targets, held)):
        step = source.shape[0] // pieces[i]
        for k in range(pieces[i]):
            at = pl.ds(k * step, step)
            spot = len(loads)
            loads.append(pltpu.make_async_copy(source.at[at], room.at[at], sem.at[0, spot]))
            stores.append(pltpu.make_async_copy(room.at[at], target.at[at], sem.at[1, spot]))
    for load in loads:
        load.start()
    for load, store in zip(loads, stores):
        load.wait()
        store.start()
    for store in stores:
        store.wait()


def hand_over(*arrays):
    pieces = (4, 1)
    hbm = pl.BlockSpec(memory_space=pltpu.HBM)
    return pl.pallas_call(
        functools.partial(passing, pieces),
        out_shape=tuple(jax.ShapeDtypeStruct(a.shape, a.dtype) for a in arrays),
        in_specs=[hbm] * len(arrays),
        out_specs=(hbm,) * len(arrays),
        scratch_shapes=[pltpu.VMEM(a.shape, a.dtype) for a in arrays]
        + [pltpu.SemaphoreType.DMA((2, sum(pieces)))],
        compiler_params=pltpu.CompilerParams(vmem_limit_bytes=66200000),
    )(*arrays)


def on_device(sizes, queries, latent_rows, segments, owners, absorb_key, absorb_value):
    n, cores = sizes
    rows = latent_rows.shape[0]
    width = LATENT + ROPE
    heads = absorb_key.shape[0]
    tokens = segments.shape[0]
    back = min(n - 1, cdiv(tokens // 2 - 1, rows))
    slots = max(2, 2 * rows // (n * cores))
    chunk = heads
    frequency = 10000.0 ** (-np.arange(ROPE // 2, dtype=np.float32) * 2.0 / ROPE)
    frequency = np.tile(frequency.astype(np.float32), 4)[None, :]
    segment_rows = segments.reshape(n, rows)
    owner_rows = owners.reshape(1, rows)
    vmem = pl.BlockSpec(memory_space=pltpu.VMEM)
    hbm = pl.BlockSpec(memory_space=pltpu.HBM)
    dma = pltpu.SemaphoreType.DMA
    results = pl.pallas_call(
        functools.partial(kernel, n, cores, back, slots, chunk),
        out_shape=(
            jax.ShapeDtypeStruct((rows, heads * VDIM), jnp.bfloat16),
            jax.ShapeDtypeStruct((1, n, slots, width), jnp.bfloat16),
        ),
        in_specs=[vmem, hbm, hbm, hbm, hbm, hbm, hbm],
        out_specs=(vmem, vmem),
        scratch_shapes=[
            pltpu.VMEM(queries.shape, jnp.bfloat16),
            pltpu.VMEM(absorb_key.shape, jnp.bfloat16),
            pltpu.VMEM(absorb_value.shape, jnp.bfloat16),
            pltpu.VMEM((heads, rows, width), jnp.bfloat16),
            pltpu.VMEM((heads * rows, LATENT), jnp.float32),
            pltpu.VMEM((heads * rows, 1), jnp.float32),
            pltpu.VMEM((heads * rows, 1), jnp.float32),
            pltpu.VMEM((n, width, rows), jnp.bfloat16),
            pltpu.VMEM((2 * rows, LATENT), jnp.bfloat16),
            pltpu.VMEM((n, 1, rows), jnp.int32),
            pltpu.VMEM((n, rows), jnp.int32),
            pltpu.VMEM((n, slots, width), jnp.bfloat16),
            dma((6,)),
            dma((n,)),
            dma((n,)),
            dma((n, cores)),
            dma((n, cores)),
            dma((n,)),
            dma((n,)),
            dma((n,)),
            dma((n,)),
        ],
        compiler_params=pltpu.CompilerParams(
            collective_id=0, has_side_effects=True, vmem_limit_bytes=66200000
        ),
    )(frequency, segment_rows, owner_rows, latent_rows.T, queries, absorb_key, absorb_value)
    return tuple(hand_over(*results))


def solution(mesh):
    in_specs = (
        P(("group", "ctx"), ("head", "dec")),
        P(("group", "ctx"), None),
        P("group"),
        P(("group", "ctx"), None),
        P(("head", "dec"), None, None),
        P(("head", "dec"), None, None),
    )
    out_specs = (P(("group", "ctx"), ("head", "dec")), P(("group", "ctx", "dec"), None, None, None))
    sizes = (mesh.shape["ctx"], mesh.shape["dec"])
    return jax.shard_map(
        functools.partial(on_device, sizes),
        mesh=mesh, in_specs=in_specs, out_specs=out_specs, check_vma=False,
    )
```
